1024 devices in a mesh: seq: 64 (over z, y), tp: 16 (over x, core).
Axes of the slice: x: 8, y: 8, z: 8, core: 2. Of those that a mesh axis runs over, the one named last changes fastest.
Arguments:
- queries: bfloat16 [8192, 2048], P('seq', 'tp'), may hold values from -4.5 to 4.5
- keys: bfloat16 [8192, 2048], P('seq', 'tp'), may hold values from -4.5 to 4.5
- values: bfloat16 [8192, 2048], P('seq', 'tp'), may hold values from -6 to 6
- step_rate: float32 [16], P('tp'), may hold values from 0.00390625 to 0.125
- memory_init: float32 [16, 128, 128], P('tp'), may hold values from -0.5 to 0.5
- out_weight: bfloat16 [2048, 2048], P('tp'), may hold values from -0.125 to 0.125
Outputs:
- layer_out: bfloat16 [8192, 2048], P('seq', 'tp')
The draws below stay inside these ranges and needn't reach their ends.
All inputs are finite; a program needn't handle non-finite values.
Results may differ from the reference program's by a relative error of at most 0.018.
Values may be sent and summed in bfloat16 or wider, within the bound.
A program may use at most 32 MiB of HBM per device.

```python
import math
import jax
import jax.numpy as jnp
from jax import lax

H = 16
HD = 128
D = 2048
WIN = 1024
CH = 16
TOKENS = 8192


def paired_rows(key):
    width = H * HD
    queries_out = jnp.clip(jax.random.normal(jax.random.fold_in(key, 201), (TOKENS, width), jnp.float32), -4.5, 4.5)
    keys_out = jnp.clip(jax.random.normal(jax.random.fold_in(key, 202), (TOKENS, width), jnp.float32), -4.5, 4.5)
    return (queries_out, keys_out)


def draw_queries(key, part):
    return paired_rows(key)[0].astype(jnp.bfloat16)


def draw_keys(key, part):
    return paired_rows(key)[1].astype(jnp.bfloat16)


def level_of(rng, extent, split, low, high):
    level = 1.0
    for axis_at, shards_of in split:
        heights = jax.random.uniform(jax.random.fold_in(jax.random.fold_in(rng, 6), axis_at), (shards_of,), jnp.float32, low / len(split), high / len(split))
        level = level * jnp.repeat(jnp.exp(heights), extent[axis_at] // shards_of).reshape((-1,) + (1,) * (len(extent) - 1 - axis_at))
    return level


def centred(stream_key, shape, scale, reach, shards=(), kind=jnp.bfloat16):
    values = jax.random.normal(stream_key, shape, jnp.float32) * scale
    if len(shards) > 0:
        values = level_of(stream_key, shape, shards, -0.22, 0.18) * values
    return jnp.clip(values, min=-reach, max=reach).astype(kind)


def setup_inputs(seed: int = 0) -> dict:
    streams_of = jax.random.split(jax.random.key(seed), 7)
    queries = draw_queries(jax.random.fold_in(streams_of[6], 71), 0)
    keys = draw_keys(jax.random.fold_in(streams_of[6], 71), 0)
    values = centred(streams_of[2], (TOKENS, H * HD), 1.0, 6.0, ((0, 64), (1, 16)))
    step_rate = jnp.clip(jnp.exp(math.log(0.125) - 3.465736 * jax.random.uniform(streams_of[3], (H,), jnp.float32) ** level_of(streams_of[3], (H,), ((0, 16),), -0.2, 0.2)), 0.00390625, 0.125)
    memory_init = centred(streams_of[4], (H, HD, HD), HD ** -0.5, 0.5, ((0, 16),), jnp.float32)
    out_weight = centred(streams_of[5], (H * HD, D), (H * HD) ** -0.5, 0.125, ((0, 16),))
    return {"queries": queries, "keys": keys, "values": values, "step_rate": step_rate, "memory_init": memory_init, "out_weight": out_weight}


highest = lax.Precision.HIGHEST

def unit_keys(keys_float):
    mean_square = lax.optimization_barrier(jnp.mean(keys_float * keys_float, axis=-1, keepdims=True))
    return keys_float / jnp.sqrt(HD * (mean_square + 1e-06))

def reference(queries, keys, values, step_rate, memory_init, out_weight):
    q_heads = queries.reshape(TOKENS, H, HD)
    k_heads = keys.reshape(TOKENS, H, HD)
    v_heads = values.reshape(TOKENS, H, HD)
    group_count = TOKENS // CH
    query_blocks = q_heads.astype(jnp.float32).reshape(group_count, CH, H, HD)
    key_blocks = unit_keys(k_heads.astype(jnp.float32)).reshape(group_count, CH, H, HD)
    value_blocks = v_heads.astype(jnp.float32).reshape(group_count, CH, H, HD)

    def update(memory, blocks):
        query_blk, key_blk, value_blk = blocks
        readout = jnp.einsum('thi,hij->thj', query_blk, memory, precision=highest)
        errors = jnp.einsum('thi,hij->thj', key_blk, memory, precision=highest) - value_blk
        gradient = jnp.einsum('thi,thj->hij', key_blk, errors, precision=highest)
        return (memory - step_rate[:, None, None] * gradient, readout)
    final_memory, readouts = lax.scan(update, memory_init.astype(jnp.float32), (query_blocks, key_blocks, value_blocks))
    memory_read = readouts.reshape(TOKENS, H, HD)
    query_block = math.gcd(512, TOKENS)
    block_count = TOKENS // query_block
    span_len = WIN + query_block
    key_padded = jnp.concatenate([jnp.zeros((WIN, H, HD), k_heads.dtype), k_heads], axis=0)
    value_padded = jnp.concatenate([jnp.zeros((WIN, H, HD), v_heads.dtype), v_heads], axis=0)

    def attend(block_index):
        offset = (block_index * query_block).astype(jnp.int32)
        query_part = lax.dynamic_slice_in_dim(q_heads, offset, query_block, 0).astype(jnp.float32)
        key_part = lax.dynamic_slice_in_dim(key_padded, offset, span_len, 0).astype(jnp.float32)
        value_part = lax.dynamic_slice_in_dim(value_padded, offset, span_len, 0).astype(jnp.float32)
        query_pos = offset + jnp.arange(query_block, dtype=jnp.int32)
        key_pos = offset - WIN + jnp.arange(span_len, dtype=jnp.int32)
        allowed = (key_pos[None, :] <= query_pos[:, None]) & (key_pos[None, :] > query_pos[:, None] - WIN) & (key_pos[None, :] >= 0)
        scores = jnp.einsum('qhd,khd->hqk', query_part, key_part) * (1.0 / math.sqrt(HD))
        scores = jnp.where(allowed[None], scores, -jnp.inf)
        maxima = lax.optimization_barrier(jnp.max(scores, axis=-1, keepdims=True))
        expd = jnp.where(allowed[None], jnp.exp(scores - maxima), 0.0)
        totals = lax.optimization_barrier(jnp.sum(expd, axis=-1, keepdims=True))
        probs = (expd / totals).astype(jnp.bfloat16)
        return jnp.einsum('hqk,khd->qhd', probs.astype(jnp.float32), value_part)
    attended = lax.map(attend, jnp.arange(block_count, dtype=jnp.int32)).reshape(TOKENS, H, HD)
    gated = (attended * jax.nn.sigmoid(memory_read)).astype(jnp.bfloat16).reshape(TOKENS, H * HD)
    return jnp.dot(gated, out_weight, preferred_element_type=jnp.float32).astype(jnp.bfloat16)
```

```python
import functools
import math

import jax
import jax.numpy as jnp
from jax import lax
from jax.experimental import pallas as pl
from jax.experimental.pallas import tpu as pltpu
from jax.sharding import PartitionSpec as P

WIN = 1024
CH = 16
MESH = pl.DeviceIdType.MESH
F32 = jnp.float32
BF16 = jnp.bfloat16


def mm(a, b):
    return lax.dot_general(a, b, (((1,), (0,)), ((), ())), preferred_element_type=F32)


def mm_bt(a, b):
    return lax.dot_general(a, b, (((1,), (1,)), ((), ())), preferred_element_type=F32)


def mm_at(a, b):
    return lax.dot_general(a, b, (((0,), (0,)), ((), ())), preferred_element_type=F32)


def kernel(
    S, T, W,
    rate_ref, q_ref, k_ref, v_ref, init_ref, w_ref, o_ref,
    kbuf, vbuf, zbuf, gbuf, wbuf,
    kv_send, kv_recv, z_send, z_recv, g_send, g_recv, w_send, w_recv,
):
    n, hd = q_ref.shape
    X = T // 2
    NZ = S // W
    up, zup = W // 2, NZ // 2
    s, t = lax.axis_index("seq"), lax.axis_index("tp")
    x, core, z = t // 2, lax.rem(t, 2), s // W
    s_next, s_prev = lax.rem(s + 1, S), lax.rem(s + S - 1, S)
    z_next, z_prev = lax.rem(s + W, S), lax.rem(s + S - W, S)
    partner = x * 2 + 1 - core

    def peer(j, other):
        xj = lax.rem(x + j, X)
        return xj * 2 + (1 - core if other else core)

    barrier = pltpu.get_barrier_semaphore()
    near = (s_next, s_prev, z_next, z_prev)
    for dev in near:
        pl.semaphore_signal(barrier, inc=1, device_id=(dev, t), device_id_type=MESH)
    for j in range(X):
        for other in (0, 1):
            if j or other:
                pl.semaphore_signal(
                    barrier, inc=1, device_id=(s, peer(j, other)), device_id_type=MESH
                )
    pl.semaphore_wait(barrier, len(near) + T - 1)

    def send(src, dst, send_sem, recv_sem, dev):
        copy = pltpu.make_async_remote_copy(
            src_ref=src, dst_ref=dst, send_sem=send_sem, recv_sem=recv_sem,
            device_id=dev, device_id_type=MESH,
        )
        copy.start()
        return copy

    pending = []
    arrive_k, arrive_v = {}, {}

    def send_kv(src, i, dev, part):
        buf = (kbuf, vbuf)[part]
        copy = send(src, buf.at[i], kv_send.at[i, part], kv_recv.at[i, part], (dev, t))
        (arrive_k, arrive_v)[part][i] = copy
        pending.append(copy)

    for part, ref in ((0, k_ref), (1, v_ref)):
        send_kv(ref, 0, s_next, part)
        send_kv(ref, W - 1, z_next, part)

    arrive_w = {}
    order = [j for i in range(1, X // 2 + 1) for j in dict.fromkeys((i, X - i))]
    for j in [0] + order:
        for other in (0, 1):
            if j or other:
                dest = peer(j, other)
                cols = pl.ds(pl.multiple_of(dest * hd, hd), hd)
                copy = send(
                    w_ref.at[:, cols], wbuf.at[j, other],
                    w_send.at[j, other], w_recv.at[j, other], (s, dest),
                )
                arrive_w[j, other] = copy
                pending.append(copy)

    row = lax.broadcasted_iota(jnp.int32, (n, n), 0)
    col = lax.broadcasted_iota(jnp.int32, (n, n), 1)
    eye = row == col
    sizes = [CH]
    while sizes[-1] < n:
        sizes.append(sizes[-1] * 2)
    masks = [
        (row // a > col // a) & (row // (2 * a) == col // (2 * a)) for a in sizes[:-1]
    ]
    eta = rate_ref[0]

    def solve(k, v, rate):
        kf = k.astype(F32)
        r = 1.0 / jnp.sqrt(hd * (jnp.mean(kf * kf, axis=1, keepdims=True) + 1e-06))
        r_row = jnp.sum(jnp.where(eye, r, 0.0), axis=0, keepdims=True)
        low = mm_bt(k, k) * (rate * r) * r_row
        inv = jnp.where(masks[0], low, 0.0)
        for mask in masks[1:]:
            inv_b = inv.astype(BF16)
            step = jnp.where(mask, low, 0.0)
            step = step - mm(inv_b, step.astype(BF16))
            step = step - mm(step.astype(BF16), inv_b)
            inv = inv + step
        w_k = r * kf - mm((inv * r_row).astype(BF16), k)
        w_v = v.astype(F32) - mm(inv.astype(BF16), v)
        return r, r_row, w_k, w_v

    def block_map(k, v, rate):
        r, _, w_k, w_v = solve(k, v, rate)
        both = jnp.concatenate([w_k, w_v], axis=1) * (rate * r)
        return mm_at(k, both.astype(BF16))

    def compose(later, earlier, earlier_b):
        later_lin = later[:, :hd]
        flip = jnp.concatenate([earlier[:, :hd], earlier[:, hd:]], axis=1)
        return later + flip - mm(later_lin.astype(BF16), earlier_b)

    q, k_own, v_own = q_ref[...], k_ref[...], v_ref[...]
    qk = mm_bt(q, k_own)
    r, r_row, w_k, w_v = solve(k_own, v_own, eta)
    reads = jnp.where(row // CH > col // CH, qk * r_row * eta, 0.0).astype(BF16)
    read_lin = q.astype(F32) - mm(reads, w_k.astype(BF16))
    read_off = mm(reads, w_v.astype(BF16))

    newer = older = None
    for step in range(up):
        lo, hi = step, W - 1 - step
        for part, arrive in ((0, arrive_k), (1, arrive_v)):
            buf = (kbuf, vbuf)[part]
            arrive[lo].wait_recv()
            if step + 1 < up:
                send_kv(buf.at[lo], lo + 1, s_next, part)
            arrive[hi].wait_recv()
            if step + 1 < up:
                send_kv(buf.at[hi], hi - 1, s_prev, part)
        maps = []
        for i in (lo, hi):
            rate = jnp.where(s >= i + 1, eta, 0.0)
            maps.append(block_map(kbuf[i], vbuf[i], rate))
        if newer is None:
            newer, older = maps
        else:
            newer = compose(newer, maps[0], maps[0].astype(BF16))
            older = compose(maps[1], older, older.astype(BF16))
    total = compose(newer, older, older.astype(BF16))

    zbuf[0] = total.astype(BF16)
    arrive_z = {}

    def send_z(i, to, dev):
        copy = send(zbuf.at[i], zbuf.at[to], z_send.at[to], z_recv.at[to], (dev, t))
        arrive_z[to] = copy
        pending.append(copy)

    send_z(0, 1, z_next)
    if NZ - 1 > zup:
        send_z(0, NZ - 1, z_prev)

    scale = 1.0 / math.sqrt(hd)
    scores = [jnp.where(col <= row, qk * scale, -jnp.inf)]
    for i in range(W):
        part = mm_bt(q, kbuf[i]) * scale
        seen = s >= i + 1
        if i == W - 1:
            seen = seen & (col > row)
        scores.append(jnp.where(seen, part, -jnp.inf))
    top = functools.reduce(jnp.maximum, scores)
    top = jnp.max(top, axis=1, keepdims=True)
    expd = [jnp.exp(part - top) for part in scores]
    norm = 1.0 / jnp.sum(functools.reduce(jnp.add, expd), axis=1, keepdims=True)
    attended = mm((expd[0] * norm).astype(BF16), v_own)
    for i in range(W):
        attended = attended + mm((expd[i + 1] * norm).astype(BF16), vbuf[i])

    state = init_ref[0]
    for step in range(zup):
        lo, hi = step + 1, NZ - 1 - step
        arrive_z[lo].wait_recv()
        if lo < zup:
            send_z(lo, lo + 1, z_next)
        if hi > zup:
            arrive_z[hi].wait_recv()
            if hi - 1 > zup:
                send_z(hi, hi - 1, z_prev)
        for i in (lo, hi)[: 2 if hi > zup else 1]:
            got = jnp.where(z >= i, zbuf[i].astype(F32), 0.0)
            got_b = got.astype(BF16)
            if i == lo:
                total = compose(total, got, got_b)
            else:
                state = state + got[:, hd:] - mm(got_b[:, :hd], state.astype(BF16))
    state_b = state.astype(BF16)
    state = state + total[:, hd:] - mm(total[:, :hd].astype(BF16), state_b)

    state_b = state.astype(BF16)
    state_l = (state - state_b.astype(F32)).astype(BF16)
    lin_b = read_lin.astype(BF16)
    lin_l = (read_lin - lin_b.astype(F32)).astype(BF16)
    memory_read = mm(lin_b, state_b) + mm(lin_l, state_b) + mm(lin_b, state_l) + read_off
    gated = (attended * jax.nn.sigmoid(memory_read)).astype(BF16)
    gbuf[0, 0] = gated

    arrive_g = {}

    def send_g(j, to, dev):
        copy = send(gbuf.at[j, 0], gbuf.at[to], g_send.at[to], g_recv.at[to], (s, dev))
        arrive_g[to] = copy
        pending.append(copy)

    for j in order:
        send_g(0, (j, 0), peer(j, 0))
    send_g(0, (0, 1), partner)

    mine = w_ref[:, pl.ds(pl.multiple_of(t * hd, hd), hd)]
    out = mm(gated, mine)
    for copy in arrive_w.values():
        copy.wait_recv()
    for j in order:
        arrive_g[j, 0].wait_recv()
        send_g(j, (j, 1), partner)
        out = out + mm(gbuf[j, 0], wbuf[j, 0])
    for j in [0] + order:
        arrive_g[j, 1].wait_recv()
        out = out + mm(gbuf[j, 1], wbuf[j, 1])
    o_ref[...] = out.astype(o_ref.dtype)
    for copy in pending:
        copy.wait_send()


def solution(mesh):
    S, T = mesh.shape["seq"], mesh.shape["tp"]

    def step(queries, keys, values, step_rate, memory_init, out_weight):
        n, hd = queries.shape
        W = WIN // n
        X, NZ = T // 2, S // W
        vmem = pl.BlockSpec(memory_space=pltpu.VMEM)
        return pl.pallas_call(
            functools.partial(kernel, S, T, W),
            out_shape=jax.ShapeDtypeStruct((n, hd), jnp.bfloat16),
            in_specs=[pl.BlockSpec(memory_space=pltpu.SMEM)] + [vmem] * 5,
            out_specs=vmem,
            scratch_shapes=[
                pltpu.VMEM((W, n, hd), BF16),
                pltpu.VMEM((W, n, hd), BF16),
                pltpu.VMEM((NZ, hd, 2 * hd), BF16),
                pltpu.VMEM((X, 2, n, hd), BF16),
                pltpu.VMEM((X, 2, hd, hd), BF16),
                pltpu.SemaphoreType.DMA((W, 2)),
                pltpu.SemaphoreType.DMA((W, 2)),
                pltpu.SemaphoreType.DMA((NZ,)),
                pltpu.SemaphoreType.DMA((NZ,)),
                pltpu.SemaphoreType.DMA((X, 2)),
                pltpu.SemaphoreType.DMA((X, 2)),
                pltpu.SemaphoreType.DMA((X, 2)),
                pltpu.SemaphoreType.DMA((X, 2)),
            ],
            compiler_params=pltpu.CompilerParams(collective_id=0, has_side_effects=True),
        )(step_rate, queries, keys, values, memory_init, out_weight)

    return jax.shard_map(
        step,
        mesh=mesh,
        in_specs=(
            P("seq", "tp"),
            P("seq", "tp"),
            P("seq", "tp"),
            P("tp"),
            P("tp", None, None),
            P("tp", None),
        ),
        out_specs=P("seq", "tp"),
        check_vma=False,
    )
```

```python
import functools
import math

import jax
import jax.numpy as jnp
from jax import lax
from jax.experimental import pallas as pl
from jax.experimental.pallas import tpu as pltpu
from jax.sharding import PartitionSpec as P

WIN = 1024
CH = 16
MESH = pl.DeviceIdType.MESH
F32 = jnp.float32
BF16 = jnp.bfloat16


def mm(a, b):
    return lax.dot_general(a, b, (((1,), (0,)), ((), ())), preferred_element_type=F32)


def mm_bt(a, b):
    return lax.dot_general(a, b, (((1,), (1,)), ((), ())), preferred_element_type=F32)


def mm_at(a, b):
    return lax.dot_general(a, b, (((0,), (0,)), ((), ())), preferred_element_type=F32)


def kernel(
    S, T, W,
    rate_ref, q_hbm, k_hbm, v_hbm, init_hbm, w_hbm, o_ref,
    q_ref, k_ref, v_ref, state_ref, own_w, kbuf, vbuf, map_out, map_in, m_out, m_in,
    gbuf, wbuf,
    in_sem, ready, kv_send, kv_recv, m_send, m_recv, g_send, g_recv, w_send, w_recv,
):
    n, hd = q_ref.shape
    X, half = T // 2, W // 2
    s, t = lax.axis_index("seq"), lax.axis_index("tp")
    x, core = t // 2, lax.rem(t, 2)
    z, y = s // W, lax.rem(s, W)
    partner = x * 2 + 1 - core

    def peer(j, other):
        xj = lax.rem(x + j, X)
        return xj * 2 + (1 - core if other else core)

    def cols(dest):
        return pl.ds(pl.multiple_of(dest * hd, hd), hd)

    def signal(sem, dev):
        pl.semaphore_signal(sem, inc=1, device_id=dev, device_id_type=MESH)

    barrier = pltpu.get_barrier_semaphore()
    wrap = range(half + 1, W)
    cross = [d for i in range(1, half + 1) for d in dict.fromkeys((i, W - i))]
    row_links = [(1, y + 1 < W), (-1, y >= 1)]
    row_links += [(d, y + d < W) for d in wrap] + [(-d, y >= d) for d in wrap]
    next_links = [(W, s + W < S), (2 * W, s + 2 * W < S)]
    next_links += [(d, (y + d >= W) & (s + d < S)) for d in cross]
    for d, there in row_links + next_links:

        @pl.when(there)
        def _():
            signal(barrier, (s + d, t))

    for j in range(X):
        for other in (0, 1):
            if j or other:
                signal(barrier, (s, peer(j, other)))

    loads = [
        pltpu.make_async_copy(src, dst, in_sem.at[i])
        for i, (src, dst) in enumerate(
            (
                (k_hbm, k_ref),
                (v_hbm, v_ref),
                (q_hbm, q_ref),
                (init_hbm.at[0], state_ref),
                (w_hbm.at[:, cols(t)], own_w),
            )
        )
    ]
    for load in loads:
        load.start()

    for yy in range(W):
        in_row = (yy + 1 < W) + (yy >= 1)
        in_row += sum((yy + d < W) + (yy >= d) for d in wrap)
        earlier = 1 + sum(yy < d for d in cross)
        for zz, more in enumerate((0, earlier, earlier + 1)):

            @pl.when((y == yy) & (z == zz if zz < 2 else z >= 2))
            def _():
                pl.semaphore_wait(barrier, T - 1 + in_row + more)

    @pl.when(z >= 1)
    def _():
        signal(ready.at[0], (s - W, t))

    @pl.when(z >= 2)
    def _():
        signal(ready.at[W], (s - 2 * W, t))

    for d in cross:

        @pl.when((y < d) & (z >= 1))
        def _():
            signal(ready.at[d], (s - d, t))

    def copy_to(src, dst, send_sem, recv_sem, dev):
        return pltpu.make_async_remote_copy(
            src_ref=src, dst_ref=dst, send_sem=send_sem, recv_sem=recv_sem,
            device_id=dev, device_id_type=MESH,
        )

    sent = []

    def kv_send_to(src, d, part, dev, there):
        i = sum(p == part for p, _, _ in sent)
        dst = (kbuf, vbuf)[part].at[d - 1]

        def make():
            return copy_to(src, dst, kv_send.at[i, part], kv_recv.at[d - 1, part], (dev, t))

        @pl.when(there)
        def _():
            make().start()

        sent.append((part, make, there))

    def kv_arrive(d, part):
        buf = (kbuf, vbuf)[part].at[d - 1]
        return copy_to(
            buf, buf, kv_send.at[0, part], kv_recv.at[d - 1, part], (lax.rem(s + 1, S), t)
        )

    for part, src in ((0, k_hbm), (1, v_hbm)):
        kv_send_to(src, 1, part, s + 1, y + 1 < W)
    for d in wrap:
        for part, src in ((0, k_hbm), (1, v_hbm)):
            kv_send_to(src, d, part, s + d, y + d < W)

    order = [j for i in range(1, X // 2 + 1) for j in dict.fromkeys((i, X - i))]
    w_copies, g_copies = {}, {}
    for j in [0] + order:
        for other in (0, 1):
            if j or other:
                dest = peer(j, other)
                copy = copy_to(
                    w_hbm.at[:, cols(dest)], wbuf.at[j, other],
                    w_send.at[j, other], w_recv.at[j, other], (s, dest),
                )
                copy.start()
                w_copies[j, other] = copy

    row = lax.broadcasted_iota(jnp.int32, (n, n), 0)
    col = lax.broadcasted_iota(jnp.int32, (n, n), 1)
    eye = row == col
    sizes = [CH]
    while sizes[-1] < n:
        sizes.append(sizes[-1] * 2)
    masks = [
        (row // a > col // a) & (row // (2 * a) == col // (2 * a)) for a in sizes[:-1]
    ]
    eta = rate_ref[0]

    def solve(k, v, rate):
        kf = k.astype(F32)
        r = 1.0 / jnp.sqrt(hd * (jnp.mean(kf * kf, axis=1, keepdims=True) + 1e-06))
        r_row = jnp.sum(jnp.where(eye, r, 0.0), axis=0, keepdims=True)
        low = mm_bt(k, k) * (rate * r) * r_row
        inv = jnp.where(masks[0], low, 0.0)
        for mask in masks[1:]:
            inv_b = inv.astype(BF16)
            step = jnp.where(mask, low, 0.0)
            step = step - mm(inv_b, step.astype(BF16))
            step = step - mm(step.astype(BF16), inv_b)
            inv = inv + step
        w_k = r * kf - mm((inv * r_row).astype(BF16), k)
        w_v = v.astype(F32) - mm(inv.astype(BF16), v)
        return r, r_row, w_k, w_v

    def block_map(k, v, rate):
        r, _, w_k, w_v = solve(k, v, rate)
        both = jnp.concatenate([w_k, w_v], axis=1) * (rate * r)
        return mm_at(k, both.astype(BF16))

    def compose(later, earlier, earlier_b):
        later_lin = later[:, :hd]
        flip = jnp.concatenate([earlier[:, :hd], earlier[:, hd:]], axis=1)
        return later + flip - mm(later_lin.astype(BF16), earlier_b)

    for load in loads:
        load.wait()
    q, k_own, v_own = q_ref[...], k_ref[...], v_ref[...]
    qk = mm_bt(q, k_own)
    r, r_row, w_k, w_v = solve(k_own, v_own, eta)
    reads = jnp.where(row // CH > col // CH, qk * r_row * eta, 0.0).astype(BF16)
    read_lin = q.astype(F32) - mm(reads, w_k.astype(BF16))
    read_off = mm(reads, w_v.astype(BF16))

    @pl.when(s + W < S)
    def _():
        pl.semaphore_wait(ready.at[0], 1)

    for part, src in ((0, k_hbm), (1, v_hbm)):
        kv_send_to(src, W, part, s + W, s + W < S)
    for d in cross:
        there = (y + d >= W) & (s + d < S)

        @pl.when(there)
        def _():
            pl.semaphore_wait(ready.at[d], 1)

        for part, src in ((0, k_hbm), (1, v_hbm)):
            kv_send_to(src, d, part, s + d, there)

    newer = older = None
    for step in range(half):
        lo, hi = step + 1, W - step
        for part, buf in ((0, kbuf), (1, vbuf)):
            for d in (lo, hi):

                @pl.when(s >= d)
                def _():
                    kv_arrive(d, part).wait_recv()

                @pl.when(s < d)
                def _():
                    buf[d - 1] = jnp.zeros((n, hd), BF16)

                src = buf.at[d - 1]
                if d == lo and lo < half:
                    kv_send_to(src, d + 1, part, s + 1, (y >= d) & (y + 1 < W))
        maps = [block_map(kbuf[d - 1], vbuf[d - 1], eta) for d in (lo, hi)]
        if newer is None:
            newer, older = maps
        else:
            newer = compose(newer, maps[0], maps[0].astype(BF16))
            older = compose(maps[1], older, older.astype(BF16))
    total = compose(newer, older, older.astype(BF16))

    def map_copy():
        return copy_to(map_out, map_in, m_send.at[0], m_recv.at[0], (lax.rem(s + W, S), t))

    def m_copy():
        return copy_to(m_out, m_in, m_send.at[1], m_recv.at[1], (lax.rem(s + 2 * W, S), t))

    map_out[...] = total.astype(BF16)

    @pl.when(s + W < S)
    def _():
        map_copy().start()

    scale = 1.0 / math.sqrt(hd)
    scores = [jnp.where(col <= row, qk * scale, -jnp.inf)]
    for i in range(W):
        part = mm_bt(q, kbuf[i]) * scale
        seen = s >= i + 1
        if i == W - 1:
            seen = seen & (col > row)
        scores.append(jnp.where(seen, part, -jnp.inf))
    top = functools.reduce(jnp.maximum, scores)
    top = jnp.max(top, axis=1, keepdims=True)
    expd = [jnp.exp(part - top) for part in scores]
    norm = 1.0 / jnp.sum(functools.reduce(jnp.add, expd), axis=1, keepdims=True)
    attended = mm((expd[0] * norm).astype(BF16), v_own)
    for i in range(W):
        attended = attended + mm((expd[i + 1] * norm).astype(BF16), vbuf[i])

    @pl.when(z >= 1)
    def _():
        map_copy().wait_recv()

    @pl.when(z < 1)
    def _():
        map_in[...] = jnp.zeros((hd, 2 * hd), BF16)

    before = map_in[...]
    total = compose(total, before.astype(F32), before)

    @pl.when(z >= 2)
    def _():
        m_copy().wait_recv()
        state_ref[...] = m_in[...].astype(F32)

    state = state_ref[...]
    state = state + total[:, hd:] - mm(total[:, :hd].astype(BF16), state.astype(BF16))
    state_b = state.astype(BF16)
    m_out[...] = state_b

    @pl.when(s + 2 * W < S)
    def _():
        pl.semaphore_wait(ready.at[W], 1)
        m_copy().start()

    state_l = (state - state_b.astype(F32)).astype(BF16)
    lin_b = read_lin.astype(BF16)
    lin_l = (read_lin - lin_b.astype(F32)).astype(BF16)
    memory_read = mm(lin_b, state_b) + mm(lin_l, state_b) + mm(lin_b, state_l) + read_off
    gated = (attended * jax.nn.sigmoid(memory_read)).astype(BF16)
    gbuf[0, 0] = gated

    def send_g(j, to, dev):
        copy = copy_to(gbuf.at[j, 0], gbuf.at[to], g_send.at[to], g_recv.at[to], (s, dev))
        copy.start()
        g_copies[to] = copy

    for j in order:
        send_g(0, (j, 0), peer(j, 0))
    send_g(0, (0, 1), partner)

    out = mm(gated, own_w[...])
    for copy in w_copies.values():
        copy.wait_recv()
    for j in order:
        g_copies[j, 0].wait_recv()
        send_g(j, (j, 1), partner)
        out = out + mm(gbuf[j, 0], wbuf[j, 0])
    for j in [0] + order:
        g_copies[j, 1].wait_recv()
        out = out + mm(gbuf[j, 1], wbuf[j, 1])
    o_ref[...] = out.astype(o_ref.dtype)

    for _, make, there in sent:

        @pl.when(there)
        def _():
            make().wait_send()

    @pl.when(s + W < S)
    def _():
        map_copy().wait_send()

    @pl.when(s + 2 * W < S)
    def _():
        m_copy().wait_send()

    for copy in [*w_copies.values(), *g_copies.values()]:
        copy.wait_send()


def solution(mesh):
    S, T = mesh.shape["seq"], mesh.shape["tp"]

    def step(queries, keys, values, step_rate, memory_init, out_weight):
        n, hd = queries.shape
        W = WIN // n
        X = T // 2
        dma = pltpu.SemaphoreType.DMA
        anywhere = pl.BlockSpec(memory_space=pl.ANY)
        return pl.pallas_call(
            functools.partial(kernel, S, T, W),
            out_shape=jax.ShapeDtypeStruct((n, hd), jnp.bfloat16),
            in_specs=[pl.BlockSpec(memory_space=pltpu.SMEM)] + [anywhere] * 5,
            out_specs=pl.BlockSpec(memory_space=pltpu.VMEM),
            scratch_shapes=[
                pltpu.VMEM((n, hd), BF16),
                pltpu.VMEM((n, hd), BF16),
                pltpu.VMEM((n, hd), BF16),
                pltpu.VMEM((hd, hd), F32),
                pltpu.VMEM((hd, hd), BF16),
                pltpu.VMEM((W, n, hd), BF16),
                pltpu.VMEM((W, n, hd), BF16),
                pltpu.VMEM((hd, 2 * hd), BF16),
                pltpu.VMEM((hd, 2 * hd), BF16),
                pltpu.VMEM((hd, hd), BF16),
                pltpu.VMEM((hd, hd), BF16),
                pltpu.VMEM((X, 2, n, hd), BF16),
                pltpu.VMEM((X, 2, hd, hd), BF16),
                dma((5,)),
                pltpu.SemaphoreType.REGULAR((W + 1,)),
                dma((3 * W, 2)),
                dma((W, 2)),
                dma((2,)),
                dma((2,)),
                dma((X, 2)),
                dma((X, 2)),
                dma((X, 2)),
                dma((X, 2)),
            ],
            compiler_params=pltpu.CompilerParams(collective_id=0, has_side_effects=True),
        )(step_rate, queries, keys, values, memory_init, out_weight)

    return jax.shard_map(
        step,
        mesh=mesh,
        in_specs=(
            P("seq", "tp"),
            P("seq", "tp"),
            P("seq", "tp"),
            P("tp"),
            P("tp", None, None),
            P("tp", None),
        ),
        out_specs=P("seq", "tp"),
        check_vma=False,
    )
```

```python
import functools
import math

import jax
import jax.numpy as jnp
from jax import lax
from jax.experimental import pallas as pl
from jax.experimental.pallas import tpu as pltpu
from jax.sharding import PartitionSpec as P

WIN = 1024
CH = 16
MESH = pl.DeviceIdType.MESH
F32 = jnp.float32
BF16 = jnp.bfloat16


def mm(a, b):
    return lax.dot_general(a, b, (((1,), (0,)), ((), ())), preferred_element_type=F32)


def mm_bt(a, b):
    return lax.dot_general(a, b, (((1,), (1,)), ((), ())), preferred_element_type=F32)


def mm_at(a, b):
    return lax.dot_general(a, b, (((0,), (0,)), ((), ())), preferred_element_type=F32)


def kernel(
    S, T, W,
    rate_ref, q_hbm, k_hbm, v_hbm, init_hbm, w_hbm, o_ref,
    q_ref, k_ref, v_ref, state_ref, own_w, kbuf, vbuf, map_out, map_in, m_out, m_in,
    near_ref, far_ref, gbuf, wbuf,
    in_sem, ready, kv_send, kv_recv, m_send, m_recv, g_send, g_recv, w_send, w_recv,
):
    n, hd = q_ref.shape
    X, half = T // 2, W // 2
    s, t = lax.axis_index("seq"), lax.axis_index("tp")
    x, core = t // 2, lax.rem(t, 2)
    z, y = s // W, lax.rem(s, W)
    partner = x * 2 + 1 - core

    def peer(j, other):
        xj = lax.rem(x + j, X)
        return xj * 2 + (1 - core if other else core)

    def cols(dest):
        return pl.ds(pl.multiple_of(dest * hd, hd), hd)

    def signal(sem, dev):
        pl.semaphore_signal(sem, inc=1, device_id=dev, device_id_type=MESH)

    barrier = pltpu.get_barrier_semaphore()
    reach = min(half, 2)
    direct = [*range(1, reach + 1), *range(half + 1, W)]
    cross = range(1, W)
    row_links = [(d, y + d < W) for d in direct] + [(-d, y >= d) for d in direct]
    next_links = [(W, s + W < S), (2 * W, s + 2 * W < S)]
    next_links += [(d, (y + d >= W) & (s + d < S)) for d in cross]
    for d, there in row_links + next_links:

        @pl.when(there)
        def _():
            signal(barrier, (s + d, t))

    for j in range(X):
        for other in (0, 1):
            if j or other:
                signal(barrier, (s, peer(j, other)))

    loads = [
        pltpu.make_async_copy(src, dst, in_sem.at[i])
        for i, (src, dst) in enumerate(
            (
                (k_hbm, k_ref),
                (v_hbm, v_ref),
                (q_hbm, q_ref),
                (init_hbm.at[0], state_ref),
                (w_hbm.at[:, cols(t)], own_w),
            )
        )
    ]
    for load in loads:
        load.start()

    for yy in range(W):
        in_row = sum((yy + d < W) + (yy >= d) for d in direct)
        earlier = 1 + sum(yy < d for d in cross)
        for zz, more in enumerate((0, earlier, earlier + 1)):

            @pl.when((y == yy) & (z == zz if zz < 2 else z >= 2))
            def _():
                pl.semaphore_wait(barrier, T - 1 + in_row + more)

    @pl.when(z >= 1)
    def _():
        signal(ready.at[0], (s - W, t))

    @pl.when(z >= 2)
    def _():
        signal(ready.at[W], (s - 2 * W, t))

    for d in cross:

        @pl.when((y < d) & (z >= 1))
        def _():
            signal(ready.at[d], (s - d, t))

    def copy_to(src, dst, send_sem, recv_sem, dev):
        return pltpu.make_async_remote_copy(
            src_ref=src, dst_ref=dst, send_sem=send_sem, recv_sem=recv_sem,
            device_id=dev, device_id_type=MESH,
        )

    sent = []

    def kv_send_to(src, d, part, dev, there):
        i = sum(p == part for p, _, _ in sent)
        dst = (kbuf, vbuf)[part].at[d - 1]

        def make():
            return copy_to(src, dst, kv_send.at[i, part], kv_recv.at[d - 1, part], (dev, t))

        @pl.when(there)
        def _():
            make().start()

        sent.append((part, make, there))

    def kv_arrive(d, part):
        buf = (kbuf, vbuf)[part].at[d - 1]
        return copy_to(
            buf, buf, kv_send.at[0, part], kv_recv.at[d - 1, part], (lax.rem(s + 1, S), t)
        )

    for d in direct:
        for part, src in ((0, k_hbm), (1, v_hbm)):
            kv_send_to(src, d, part, s + d, y + d < W)

    order = [j for i in range(1, X // 2 + 1) for j in dict.fromkeys((i, X - i))]
    w_copies, g_copies = {}, {}
    for j in [0] + order:
        for other in (0, 1):
            if j or other:
                dest = peer(j, other)
                copy = copy_to(
                    w_hbm.at[:, cols(dest)], wbuf.at[j, other],
                    w_send.at[j, other], w_recv.at[j, other], (s, dest),
                )
                copy.start()
                w_copies[j, other] = copy

    row = lax.broadcasted_iota(jnp.int32, (n, n), 0)
    col = lax.broadcasted_iota(jnp.int32, (n, n), 1)
    eye = row == col
    sizes = [CH]
    while sizes[-1] < n:
        sizes.append(sizes[-1] * 2)
    masks = [
        (row // a > col // a) & (row // (2 * a) == col // (2 * a)) for a in sizes[:-1]
    ]
    eta = rate_ref[0]

    def solve(k, v, rate):
        kf = k.astype(F32)
        r = 1.0 / jnp.sqrt(hd * (jnp.mean(kf * kf, axis=1, keepdims=True) + 1e-06))
        r_row = jnp.sum(jnp.where(eye, r, 0.0), axis=0, keepdims=True)
        low = mm_bt(k, k) * (rate * r) * r_row
        inv = jnp.where(masks[0], low, 0.0)
        for mask in masks[1:]:
            inv_b = inv.astype(BF16)
            step = jnp.where(mask, low, 0.0)
            step = step - mm(inv_b, step.astype(BF16))
            step = step - mm(step.astype(BF16), inv_b)
            inv = inv + step
        w_k = r * kf - mm((inv * r_row).astype(BF16), k)
        w_v = v.astype(F32) - mm(inv.astype(BF16), v)
        return r, r_row, w_k, w_v

    def block_map(k, v, rate):
        r, _, w_k, w_v = solve(k, v, rate)
        both = jnp.concatenate([w_k, w_v], axis=1) * (rate * r)
        return mm_at(k, both.astype(BF16))

    def compose(later, earlier, earlier_b):
        later_lin = later[:, :hd]
        flip = jnp.concatenate([earlier[:, :hd], earlier[:, hd:]], axis=1)
        return later + flip - mm(later_lin.astype(BF16), earlier_b)

    def send_later(now):
        for d in range(1, W + 1):
            there = (y + d >= W) & (s + d < S) & now(d)

            @pl.when(there)
            def _():
                pl.semaphore_wait(ready.at[d % W], 1)

            for part, src in ((0, k_hbm), (1, v_hbm)):
                kv_send_to(src, d, part, s + d, there)

    for load in loads:
        load.wait()
    q, k_own, v_own = q_ref[...], k_ref[...], v_ref[...]
    qk = mm_bt(q, k_own)
    r, r_row, w_k, w_v = solve(k_own, v_own, eta)
    reads = jnp.where(row // CH > col // CH, qk * r_row * eta, 0.0).astype(BF16)
    read_lin = q.astype(F32) - mm(reads, w_k.astype(BF16))
    read_off = mm(reads, w_v.astype(BF16))

    send_later(lambda d: (y + d < W + half) & (d <= half))
    if half > reach:
        for part, buf in ((0, kbuf), (1, vbuf)):

            @pl.when((y >= reach) & (y + 1 < W))
            def _():
                kv_arrive(reach, part).wait_recv()

            for d in range(reach + 1, half + 1):
                hop = d - reach
                there = (y >= reach) & (y + hop < W)
                kv_send_to(buf.at[reach - 1], d, part, s + hop, there)
    send_later(lambda d: d > half)

    def maps_of(distances):
        return [block_map(kbuf[d - 1], vbuf[d - 1], eta) for d in distances]

    def join(maps):
        return functools.reduce(lambda p, m: compose(p, m, m.astype(BF16)), maps)

    full = (z >= 1) | (y > half)
    for first in range(half):
        steps = range(first, first + 1)
        near, far = [i + 1 for i in steps], [W - i for i in steps][::-1]
        for step in steps:
            lo, hi = step + 1, W - step
            for part, buf in ((0, kbuf), (1, vbuf)):
                for d in (lo, hi):

                    @pl.when((s >= d) & ((y < d) | (y + 1 >= W)) if d == reach < half else s >= d)
                    def _():
                        kv_arrive(d, part).wait_recv()

                    @pl.when(s < d)
                    def _():
                        buf[d - 1] = jnp.zeros((n, hd), BF16)

        @pl.when(full)
        def _():
            maps = maps_of(near + far)
            newer, older = join(maps[: len(near)]), join(maps[len(near) :])
            if first:
                newer = compose(near_ref[...], newer, newer.astype(BF16))
                earlier = far_ref[...]
                older = compose(older, earlier, earlier.astype(BF16))
            near_ref[...] = newer
            far_ref[...] = older

        @pl.when((z == 0) & (y <= half) & (y >= near[0]))
        def _():
            newer = join(maps_of(near))
            if first:
                newer = compose(near_ref[...], newer, newer.astype(BF16))
            else:
                far_ref[...] = jnp.zeros((hd, 2 * hd), F32)
            near_ref[...] = newer

        if not first:

            @pl.when(s == 0)
            def _():
                near_ref[...] = jnp.zeros((hd, 2 * hd), F32)
                far_ref[...] = jnp.zeros((hd, 2 * hd), F32)

    older = far_ref[...]
    total = compose(near_ref[...], older, older.astype(BF16))

    def map_copy():
        return copy_to(map_out, map_in, m_send.at[0], m_recv.at[0], (lax.rem(s + W, S), t))

    def m_copy():
        return copy_to(m_out, m_in, m_send.at[1], m_recv.at[1], (lax.rem(s + 2 * W, S), t))

    map_out[...] = total.astype(BF16)

    @pl.when(s + W < S)
    def _():
        map_copy().start()

    scale = 1.0 / math.sqrt(hd)
    scores = [jnp.where(col <= row, qk * scale, -jnp.inf)]
    for i in range(W):
        part = mm_bt(q, kbuf[i]) * scale
        seen = s >= i + 1
        if i == W - 1:
            seen = seen & (col > row)
        scores.append(jnp.where(seen, part, -jnp.inf))
    top = functools.reduce(jnp.maximum, scores)
    top = jnp.max(top, axis=1, keepdims=True)
    expd = [jnp.exp(part - top) for part in scores]
    norm = 1.0 / jnp.sum(functools.reduce(jnp.add, expd), axis=1, keepdims=True)
    attended = mm((expd[0] * norm).astype(BF16), v_own)
    for i in range(W):
        attended = attended + mm((expd[i + 1] * norm).astype(BF16), vbuf[i])

    @pl.when(z >= 1)
    def _():
        map_copy().wait_recv()

    @pl.when(z < 1)
    def _():
        map_in[...] = jnp.zeros((hd, 2 * hd), BF16)

    before = map_in[...]
    total = compose(total, before.astype(F32), before)

    @pl.when(z >= 2)
    def _():
        m_copy().wait_recv()
        state_ref[...] = m_in[...].astype(F32)

    state = state_ref[...]
    state = state + total[:, hd:] - mm(total[:, :hd].astype(BF16), state.astype(BF16))
    state_b = state.astype(BF16)
    m_out[...] = state_b

    @pl.when(s + 2 * W < S)
    def _():
        pl.semaphore_wait(ready.at[W], 1)
        m_copy().start()

    state_l = (state - state_b.astype(F32)).astype(BF16)
    lin_b = read_lin.astype(BF16)
    lin_l = (read_lin - lin_b.astype(F32)).astype(BF16)
    memory_read = mm(lin_b, state_b) + mm(lin_l, state_b) + mm(lin_b, state_l) + read_off
    gated = (attended * jax.nn.sigmoid(memory_read)).astype(BF16)
    gbuf[0, 0] = gated

    def send_g(j, to, dev):
        copy = copy_to(gbuf.at[j, 0], gbuf.at[to], g_send.at[to], g_recv.at[to], (s, dev))
        copy.start()
        g_copies[to] = copy

    for j in order:
        send_g(0, (j, 0), peer(j, 0))
    send_g(0, (0, 1), partner)

    out = mm(gated, own_w[...])
    for copy in w_copies.values():
        copy.wait_recv()
    for j in order:
        g_copies[j, 0].wait_recv()
        send_g(j, (j, 1), partner)
        out = out + mm(gbuf[j, 0], wbuf[j, 0])
    for j in [0] + order:
        g_copies[j, 1].wait_recv()
        out = out + mm(gbuf[j, 1], wbuf[j, 1])
    o_ref[...] = out.astype(o_ref.dtype)

    for _, make, there in sent:

        @pl.when(there)
        def _():
            make().wait_send()

    @pl.when(s + W < S)
    def _():
        map_copy().wait_send()

    @pl.when(s + 2 * W < S)
    def _():
        m_copy().wait_send()

    for copy in [*w_copies.values(), *g_copies.values()]:
        copy.wait_send()


def solution(mesh):
    S, T = mesh.shape["seq"], mesh.shape["tp"]

    def step(queries, keys, values, step_rate, memory_init, out_weight):
        n, hd = queries.shape
        W = WIN // n
        X = T // 2
        dma = pltpu.SemaphoreType.DMA
        anywhere = pl.BlockSpec(memory_space=pl.ANY)
        return pl.pallas_call(
            functools.partial(kernel, S, T, W),
            out_shape=jax.ShapeDtypeStruct((n, hd), jnp.bfloat16),
            in_specs=[pl.BlockSpec(memory_space=pltpu.SMEM)] + [anywhere] * 5,
            out_specs=pl.BlockSpec(memory_space=pltpu.VMEM),
            scratch_shapes=[
                pltpu.VMEM((n, hd), BF16),
                pltpu.VMEM((n, hd), BF16),
                pltpu.VMEM((n, hd), BF16),
                pltpu.VMEM((hd, hd), F32),
                pltpu.VMEM((hd, hd), BF16),
                pltpu.VMEM((W, n, hd), BF16),
                pltpu.VMEM((W, n, hd), BF16),
                pltpu.VMEM((hd, 2 * hd), BF16),
                pltpu.VMEM((hd, 2 * hd), BF16),
                pltpu.VMEM((hd, hd), BF16),
                pltpu.VMEM((hd, hd), BF16),
                pltpu.VMEM((hd, 2 * hd), F32),
                pltpu.VMEM((hd, 2 * hd), F32),
                pltpu.VMEM((X, 2, n, hd), BF16),
                pltpu.VMEM((X, 2, hd, hd), BF16),
                dma((5,)),
                pltpu.SemaphoreType.REGULAR((W + 1,)),
                dma((3 * W, 2)),
                dma((W, 2)),
                dma((2,)),
                dma((2,)),
                dma((X, 2)),
                dma((X, 2)),
                dma((X, 2)),
                dma((X, 2)),
            ],
            compiler_params=pltpu.CompilerParams(collective_id=0, has_side_effects=True),
        )(step_rate, queries, keys, values, memory_init, out_weight)

    return jax.shard_map(
        step,
        mesh=mesh,
        in_specs=(
            P("seq", "tp"),
            P("seq", "tp"),
            P("seq", "tp"),
            P("tp"),
            P("tp", None, None),
            P("tp", None),
        ),
        out_specs=P("seq", "tp"),
        check_vma=False,
    )
```

```python
import functools
import math

import jax
import jax.numpy as jnp
from jax import lax
from jax.experimental import pallas as pl
from jax.experimental.pallas import tpu as pltpu
from jax.sharding import PartitionSpec as P

WIN = 1024
CH = 16
MESH = pl.DeviceIdType.MESH
F32 = jnp.float32
BF16 = jnp.bfloat16


def mm(a, b):
    return lax.dot_general(a, b, (((1,), (0,)), ((), ())), preferred_element_type=F32)


def mm_bt(a, b):
    return lax.dot_general(a, b, (((1,), (1,)), ((), ())), preferred_element_type=F32)


def mm_at(a, b):
    return lax.dot_general(a, b, (((0,), (0,)), ((), ())), preferred_element_type=F32)


def kernel(
    S, T, W,
    rate_ref, q_hbm, k_hbm, v_hbm, init_hbm, w_hbm, o_ref,
    q_ref, k_ref, v_ref, state_ref, own_w, kbuf, vbuf, map_out, map_in, m_out, m_in,
    near_ref, far_ref, gbuf, wbuf,
    in_sem, ready, kv_send, kv_recv, m_send, m_recv, g_send, g_recv, w_send, w_recv,
):
    n, hd = q_ref.shape
    X, half = T // 2, W // 2
    s, t = lax.axis_index("seq"), lax.axis_index("tp")
    x, core = t // 2, lax.rem(t, 2)
    z, y = s // W, lax.rem(s, W)
    partner = x * 2 + 1 - core

    def peer(j, other):
        xj = lax.rem(x + j, X)
        return xj * 2 + (1 - core if other else core)

    def cols(dest):
        return pl.ds(pl.multiple_of(dest * hd, hd), hd)

    def signal(sem, dev):
        pl.semaphore_signal(sem, inc=1, device_id=dev, device_id_type=MESH)

    barrier = pltpu.get_barrier_semaphore()
    reach = min(half, 2)
    direct = [*range(1, reach + 1), *range(half + 1, W)]
    cross = range(1, W)
    row_links = [(d, y + d < W) for d in direct] + [(-d, y >= d) for d in direct]
    next_links = [(W, s + W < S), (2 * W, s + 2 * W < S)]
    next_links += [(d, (y + d >= W) & (s + d < S)) for d in cross]
    for d, there in row_links + next_links:

        @pl.when(there)
        def _():
            signal(barrier, (s + d, t))

    for j in range(X):
        for other in (0, 1):
            if j or other:
                signal(barrier, (s, peer(j, other)))

    loads = [
        pltpu.make_async_copy(src, dst, in_sem.at[i])
        for i, (src, dst) in enumerate(
            (
                (k_hbm, k_ref),
                (v_hbm, v_ref),
                (q_hbm, q_ref),
                (init_hbm.at[0], state_ref),
                (w_hbm.at[:, cols(t)], own_w),
            )
        )
    ]
    for load in loads:
        load.start()

    for yy in range(W):
        in_row = sum((yy + d < W) + (yy >= d) for d in direct)
        earlier = 1 + sum(yy < d for d in cross)
        for zz, more in enumerate((0, earlier, earlier + 1)):

            @pl.when((y == yy) & (z == zz if zz < 2 else z >= 2))
            def _():
                pl.semaphore_wait(barrier, T - 1 + in_row + more)

    @pl.when(z >= 1)
    def _():
        signal(ready.at[0], (s - W, t))

    @pl.when(z >= 2)
    def _():
        signal(ready.at[W], (s - 2 * W, t))

    for d in cross:

        @pl.when((y < d) & (z >= 1))
        def _():
            signal(ready.at[d], (s - d, t))

    def copy_to(src, dst, send_sem, recv_sem, dev):
        return pltpu.make_async_remote_copy(
            src_ref=src, dst_ref=dst, send_sem=send_sem, recv_sem=recv_sem,
            device_id=dev, device_id_type=MESH,
        )

    sent = []

    def kv_send_to(src, d, part, dev, there):
        i = sum(p == part for p, _, _ in sent)
        dst = (kbuf, vbuf)[part].at[d - 1]

        def make():
            return copy_to(src, dst, kv_send.at[i, part], kv_recv.at[d - 1, part], (dev, t))

        @pl.when(there)
        def _():
            make().start()

        sent.append((part, make, there))

    def kv_arrive(d, part):
        buf = (kbuf, vbuf)[part].at[d - 1]
        return copy_to(
            buf, buf, kv_send.at[0, part], kv_recv.at[d - 1, part], (lax.rem(s + 1, S), t)
        )

    for d in direct:
        for part, src in ((0, k_hbm), (1, v_hbm)):
            kv_send_to(src, d, part, s + d, y + d < W)

    order = [j for i in range(1, X // 2 + 1) for j in dict.fromkeys((i, X - i))]
    w_copies, g_copies = {}, {}
    for j in [0] + order:
        for other in (0, 1):
            if j or other:
                dest = peer(j, other)
                copy = copy_to(
                    w_hbm.at[:, cols(dest)], wbuf.at[j, other],
                    w_send.at[j, other], w_recv.at[j, other], (s, dest),
                )
                copy.start()
                w_copies[j, other] = copy

    row = lax.broadcasted_iota(jnp.int32, (n, n), 0)
    col = lax.broadcasted_iota(jnp.int32, (n, n), 1)
    eye = row == col
    sizes = [CH]
    while sizes[-1] < n:
        sizes.append(sizes[-1] * 2)
    masks = [
        (row // a > col // a) & (row // (2 * a) == col // (2 * a)) for a in sizes[:-1]
    ]
    eta = rate_ref[0]

    def solve(k, v, rate):
        kf = k.astype(F32)
        r = 1.0 / jnp.sqrt(hd * (jnp.mean(kf * kf, axis=1, keepdims=True) + 1e-06))
        r_row = jnp.sum(jnp.where(eye, r, 0.0), axis=0, keepdims=True)
        low = mm_bt(k, k) * (rate * r) * r_row
        inv = jnp.where(masks[0], low, 0.0)
        for mask in masks[1:]:
            inv_b = inv.astype(BF16)
            step = jnp.where(mask, low, 0.0)
            step = step - mm(inv_b, step.astype(BF16))
            step = step - mm(step.astype(BF16), inv_b)
            inv = inv + step
        w_k = r * kf - mm((inv * r_row).astype(BF16), k)
        w_v = v.astype(F32) - mm(inv.astype(BF16), v)
        return r, r_row, w_k, w_v

    def block_map(k, v, rate):
        r, _, w_k, w_v = solve(k, v, rate)
        both = jnp.concatenate([w_k, w_v], axis=1) * (rate * r)
        return mm_at(k, both.astype(BF16))

    def compose(later, earlier, earlier_b):
        later_lin = later[:, :hd]
        flip = jnp.concatenate([earlier[:, :hd], earlier[:, hd:]], axis=1)
        return later + flip - mm(later_lin.astype(BF16), earlier_b)

    def send_later(now):
        for d in range(1, W + 1):
            there = (y + d >= W) & (s + d < S) & now(d)

            @pl.when(there)
            def _():
                pl.semaphore_wait(ready.at[d % W], 1)

            for part, src in ((0, k_hbm), (1, v_hbm)):
                kv_send_to(src, d, part, s + d, there)

    for load in loads:
        load.wait()
    q, k_own, v_own = q_ref[...], k_ref[...], v_ref[...]
    qk = mm_bt(q, k_own)
    r, r_row, w_k, w_v = solve(k_own, v_own, eta)
    reads = jnp.where(row // CH > col // CH, qk * r_row * eta, 0.0).astype(BF16)
    read_lin = q.astype(F32) - mm(reads, w_k.astype(BF16))
    read_off = mm(reads, w_v.astype(BF16))

    send_later(lambda d: (y + d < W + half) & (d <= half))
    if half > reach:
        for part, buf in ((0, kbuf), (1, vbuf)):

            @pl.when((y >= reach) & (y + 1 < W))
            def _():
                kv_arrive(reach, part).wait_recv()

            for d in range(reach + 1, half + 1):
                hop = d - reach
                there = (y >= reach) & (y + hop < W)
                kv_send_to(buf.at[reach - 1], d, part, s + hop, there)
    send_later(lambda d: d > half)

    def maps_of(distances):
        return [block_map(kbuf[d - 1], vbuf[d - 1], eta) for d in distances]

    def join(maps):
        return functools.reduce(lambda p, m: compose(p, m, m.astype(BF16)), maps)

    full = (z >= 1) | (y > half)
    for first in range(half):
        steps = range(first, first + 1)
        near, far = [i + 1 for i in steps], [half + 1 + i for i in steps]
        for step in steps:
            lo, hi = step + 1, half + 1 + step
            for part, buf in ((0, kbuf), (1, vbuf)):
                for d in (lo, hi):

                    @pl.when((s >= d) & ((y < d) | (y + 1 >= W)) if d == reach < half else s >= d)
                    def _():
                        kv_arrive(d, part).wait_recv()

                    @pl.when(s < d)
                    def _():
                        buf[d - 1] = jnp.zeros((n, hd), BF16)

        @pl.when(full)
        def _():
            maps = maps_of(near + far)
            newer, older = join(maps[: len(near)]), join(maps[len(near) :])
            if first:
                newer = compose(near_ref[...], newer, newer.astype(BF16))
                older = compose(far_ref[...], older, older.astype(BF16))
            near_ref[...] = newer
            far_ref[...] = older

        @pl.when((z == 0) & (y <= half) & (y >= near[0]))
        def _():
            newer = join(maps_of(near))
            if first:
                newer = compose(near_ref[...], newer, newer.astype(BF16))
            else:
                far_ref[...] = jnp.zeros((hd, 2 * hd), F32)
            near_ref[...] = newer

        if not first:

            @pl.when(s == 0)
            def _():
                near_ref[...] = jnp.zeros((hd, 2 * hd), F32)
                far_ref[...] = jnp.zeros((hd, 2 * hd), F32)

    older = far_ref[...]
    total = compose(near_ref[...], older, older.astype(BF16))

    def map_copy():
        return copy_to(map_out, map_in, m_send.at[0], m_recv.at[0], (lax.rem(s + W, S), t))

    def m_copy():
        return copy_to(m_out, m_in, m_send.at[1], m_recv.at[1], (lax.rem(s + 2 * W, S), t))

    map_out[...] = total.astype(BF16)

    @pl.when(s + W < S)
    def _():
        map_copy().start()

    scale = 1.0 / math.sqrt(hd)
    scores = [jnp.where(col <= row, qk * scale, -jnp.inf)]
    for i in range(W):
        part = mm_bt(q, kbuf[i]) * scale
        seen = s >= i + 1
        if i == W - 1:
            seen = seen & (col > row)
        scores.append(jnp.where(seen, part, -jnp.inf))
    top = functools.reduce(jnp.maximum, scores)
    top = jnp.max(top, axis=1, keepdims=True)
    expd = [jnp.exp(part - top) for part in scores]
    norm = 1.0 / jnp.sum(functools.reduce(jnp.add, expd), axis=1, keepdims=True)
    attended = mm((expd[0] * norm).astype(BF16), v_own)
    for i in range(W):
        attended = attended + mm((expd[i + 1] * norm).astype(BF16), vbuf[i])

    @pl.when(z >= 1)
    def _():
        map_copy().wait_recv()

    @pl.when(z < 1)
    def _():
        map_in[...] = jnp.zeros((hd, 2 * hd), BF16)

    before = map_in[...]
    total = compose(total, before.astype(F32), before)

    @pl.when(z >= 2)
    def _():
        m_copy().wait_recv()
        state_ref[...] = m_in[...].astype(F32)

    state = state_ref[...]
    state = state + total[:, hd:] - mm(total[:, :hd].astype(BF16), state.astype(BF16))
    state_b = state.astype(BF16)
    m_out[...] = state_b

    @pl.when(s + 2 * W < S)
    def _():
        pl.semaphore_wait(ready.at[W], 1)
        m_copy().start()

    state_l = (state - state_b.astype(F32)).astype(BF16)
    lin_b = read_lin.astype(BF16)
    lin_l = (read_lin - lin_b.astype(F32)).astype(BF16)
    memory_read = mm(lin_b, state_b) + mm(lin_l, state_b) + mm(lin_b, state_l) + read_off
    gated = (attended * jax.nn.sigmoid(memory_read)).astype(BF16)
    gbuf[0, 0] = gated

    def send_g(j, to, dev):
        copy = copy_to(gbuf.at[j, 0], gbuf.at[to], g_send.at[to], g_recv.at[to], (s, dev))
        copy.start()
        g_copies[to] = copy

    for j in order:
        send_g(0, (j, 0), peer(j, 0))
    send_g(0, (0, 1), partner)

    out = mm(gated, own_w[...])
    for copy in w_copies.values():
        copy.wait_recv()
    for j in order:
        g_copies[j, 0].wait_recv()
        send_g(j, (j, 1), partner)
        out = out + mm(gbuf[j, 0], wbuf[j, 0])
    for j in [0] + order:
        g_copies[j, 1].wait_recv()
        out = out + mm(gbuf[j, 1], wbuf[j, 1])
    o_ref[...] = out.astype(o_ref.dtype)

    for _, make, there in sent:

        @pl.when(there)
        def _():
            make().wait_send()

    @pl.when(s + W < S)
    def _():
        map_copy().wait_send()

    @pl.when(s + 2 * W < S)
    def _():
        m_copy().wait_send()

    for copy in [*w_copies.values(), *g_copies.values()]:
        copy.wait_send()


def solution(mesh):
    S, T = mesh.shape["seq"], mesh.shape["tp"]

    def step(queries, keys, values, step_rate, memory_init, out_weight):
        n, hd = queries.shape
        W = WIN // n
        X = T // 2
        dma = pltpu.SemaphoreType.DMA
        anywhere = pl.BlockSpec(memory_space=pl.ANY)
        return pl.pallas_call(
            functools.partial(kernel, S, T, W),
            out_shape=jax.ShapeDtypeStruct((n, hd), jnp.bfloat16),
            in_specs=[pl.BlockSpec(memory_space=pltpu.SMEM)] + [anywhere] * 5,
            out_specs=pl.BlockSpec(memory_space=pltpu.VMEM),
            scratch_shapes=[
                pltpu.VMEM((n, hd), BF16),
                pltpu.VMEM((n, hd), BF16),
                pltpu.VMEM((n, hd), BF16),
                pltpu.VMEM((hd, hd), F32),
                pltpu.VMEM((hd, hd), BF16),
                pltpu.VMEM((W, n, hd), BF16),
                pltpu.VMEM((W, n, hd), BF16),
                pltpu.VMEM((hd, 2 * hd), BF16),
                pltpu.VMEM((hd, 2 * hd), BF16),
                pltpu.VMEM((hd, hd), BF16),
                pltpu.VMEM((hd, hd), BF16),
                pltpu.VMEM((hd, 2 * hd), F32),
                pltpu.VMEM((hd, 2 * hd), F32),
                pltpu.VMEM((X, 2, n, hd), BF16),
                pltpu.VMEM((X, 2, hd, hd), BF16),
                dma((5,)),
                pltpu.SemaphoreType.REGULAR((W + 1,)),
                dma((3 * W, 2)),
                dma((W, 2)),
                dma((2,)),
                dma((2,)),
                dma((X, 2)),
                dma((X, 2)),
                dma((X, 2)),
                dma((X, 2)),
            ],
            compiler_params=pltpu.CompilerParams(collective_id=0, has_side_effects=True),
        )(step_rate, queries, keys, values, memory_init, out_weight)

    return jax.shard_map(
        step,
        mesh=mesh,
        in_specs=(
            P("seq", "tp"),
            P("seq", "tp"),
            P("seq", "tp"),
            P("tp"),
            P("tp", None, None),
            P("tp", None),
        ),
        out_specs=P("seq", "tp"),
        check_vma=False,
    )
```
